512 devices in a mesh: pp: 16 (over z, core), ep: 32 (over x, y).
Axes of the slice: x: 4, y: 8, z: 8, core: 2. Of those that a mesh axis runs over, the one named last changes fastest.
Arguments:
- pending_activations: bfloat16 [16, 2048, 3584], P('pp', 'ep'), may hold values from -6 to 6
- incoming_microbatches: bfloat16 [1, 2048, 3584], P(None, 'ep'), may hold values from -6 to 6
- layer_rescale_factor: float32 [16, 3584], P('pp'), may hold values from 0.5 to 1.5
- gating_projection_matrix: bfloat16 [16, 3584, 4096], P('pp', None, 'ep'), may hold values from -0.09375 to 0.09375
- widening_projection_matrix: bfloat16 [16, 3584, 4096], P('pp', None, 'ep'), may hold values from -0.09375 to 0.09375
- output_projection_matrix: bfloat16 [16, 4096, 3584], P('pp', 'ep'), may hold values from -0.1875 to 0.1875
- picked_specialist_ids: int32 [2, 16, 2048, 1], P(None, 'pp', 'ep'), may hold values from 0 to 3; in each aligned block of 64 rows (0 to 63, 64 to 127, ..., all dimensions but the last counted through in order) at most 17 rows name the same one
- dispatcher_probability_values: float32 [2, 16, 2048, 1], P(None, 'pp', 'ep'), may hold values from 0.1 to 1
Outputs:
- section_outputs: bfloat16 [2, 16, 2048, 3584], P(None, 'pp', 'ep')
The draws below stay inside these ranges and needn't reach their ends.
Inputs may be any that keep to these rules, and one draw needn't show every extreme that they name: `picked_specialist_ids`: each token names exactly one expert. In each step and section, the 64 rows of one device (aligned blocks of the token dimension) name each expert at most 17 times, a bound that some block reaches.
All inputs are finite; a program needn't handle non-finite values.
Results may differ from the reference program's by a relative error of at most 0.0055.
Values may be sent and summed in bfloat16 or wider, within the bound.
No kernel may reach another device: no remote copies, remote signals or barrier semaphores. Data moves between devices by JAX's collectives and lax.ppermute only.
A program may use at most 64 MiB of HBM per device.

```python
import math
import jax
import jax.numpy as jnp
import numpy as np
from jax import lax

HIDDEN_SPAN = 3584
FF = 1024
GROUP = 8
TOPK = 1
ROWS = 64
TICKS = 2
LAYER_COUNT = 16
EXPERTS = 4
CAP = 17
MICRO_ITEM_COUNT = 2048
N_EP = 32


def shard_levels(stream_key, dims, cuts, low, top_value):
    level, own = 1.0, jax.random.fold_in(stream_key, 6)
    for dim, shards_of in cuts:
        steps = jnp.exp(jax.random.uniform(jax.random.fold_in(own, dim), (shards_of,), jnp.float32, low / len(cuts), top_value / len(cuts)))
        level = level * jnp.repeat(steps, dims[dim] // shards_of).reshape([-1 if axis == dim else 1 for axis in range(len(dims))])
    return level


def deal_out(rng, own, number, rows, count, top, limit, skew):
    ranking = jax.random.permutation(rng, count)
    crowded, ordinary = shares(count, rows * top, limit, skew, True), shares(count, rows * top, limit, skew, False)
    places = jnp.arange(count)

    def named(tallies, rotation):
        used = int((tallies > 0).sum())
        fixed = max(1, used // 4)
        passed = fixed + (places - fixed + rotation * (used - fixed)) % max(1, count - fixed)
        return jnp.zeros((count,), jnp.int32).at[ranking[jnp.where(places < fixed, places, passed)]].set(jnp.asarray(tallies, jnp.int32))

    tallies = jnp.where(number % 4 == 0, named(crowded, number // 4), named(ordinary, number - number // 4 - 1))
    mixed = jax.random.permutation(jax.random.fold_in(own, 3), count)
    giver, sink = mixed[0:count // 2 * 2:2], mixed[1:count // 2 * 2:2]
    margin = jnp.minimum(tallies[giver] - 1, limit - tallies[sink]) // 2
    margin = jnp.where((giver == ranking[0]) | (sink == ranking[0]) | (tallies[sink] == 0), 0, jnp.maximum(margin, 0))
    passed = jax.random.randint(jax.random.fold_in(own, 4), (count // 2,), 0, 1 << 20) % (margin + 1)
    tallies = tallies.at[giver].add(-passed).at[sink].add(passed)
    labels = jnp.searchsorted(jnp.cumsum(tallies), jnp.arange(rows * top), side="right").astype(jnp.int32)
    listing = labels.reshape(top, rows).T
    listing = listing[jax.random.permutation(jax.random.fold_in(own, 1), rows)]
    rotation = jax.random.randint(jax.random.fold_in(own, 2), (rows, 1), 0, top)
    return jnp.take_along_axis(listing, (jnp.arange(top)[None, :] + rotation) % top, axis=1)


def shares(amount, total, bound, slope, full):
    portions = [(1 << 20) // math.isqrt(rank ** slope) + 1 for rank in range(1, amount + 1)]
    largest = bound if full else min(bound, max(-(-total // amount), total * portions[0] // sum(portions)))
    least = 1 if total - largest >= amount - 1 else 0
    holding, spare = [largest] + [least] * (amount - 1), total - largest - least * (amount - 1)
    while spare > 0:
        candidates = [i for i in range(1, amount) if holding[i] < largest] or [i for i in range(1, amount) if holding[i] < bound]
        whole, remaining = sum([portions[i] for i in candidates]), spare
        for i in candidates:
            addition = min(bound - holding[i], max(1, remaining * portions[i] // whole), spare)
            holding[i] = holding[i] + addition
            spare = spare - addition
    return np.array(holding)


def normal_values(stream_key, shape, deviation, bound, pieces=(), held_as=jnp.bfloat16):
    values = deviation * jax.random.normal(stream_key, shape, jnp.float32)
    if pieces:
        values = values * shard_levels(stream_key, shape, pieces, -0.22, 0.18)
    return jnp.clip(values, -bound, bound).astype(held_as)


def setup_inputs(seed: int = 0) -> dict:
    keys = jax.random.split(jax.random.key(seed), 9)
    pending_activations = normal_values(keys[0], (LAYER_COUNT, MICRO_ITEM_COUNT, HIDDEN_SPAN), 1.0, 6.0, ((0, 16), (1, 32)))
    incoming_microbatches = normal_values(keys[1], (TICKS - 1, MICRO_ITEM_COUNT, HIDDEN_SPAN), 1.0, 6.0, ((1, 32),))
    layer_rescale_factor = jnp.clip(1.0 + 0.1 * jax.random.normal(keys[2], (LAYER_COUNT, HIDDEN_SPAN), jnp.float32), 0.5, 1.5)
    gating_projection_matrix = normal_values(keys[3], (LAYER_COUNT, HIDDEN_SPAN, EXPERTS * FF), HIDDEN_SPAN ** -0.5, 0.09375, ((0, 16), (2, 32)))
    widening_projection_matrix = normal_values(keys[4], (LAYER_COUNT, HIDDEN_SPAN, EXPERTS * FF), HIDDEN_SPAN ** -0.5, 0.09375, ((0, 16), (2, 32)))
    output_projection_matrix = normal_values(keys[5], (LAYER_COUNT, EXPERTS * FF, HIDDEN_SPAN), FF ** -0.5, 0.1875, ((0, 16), (1, 32)))
    picked_specialist_ids_keys = jax.random.split(jax.random.fold_in(keys[6], 1), TICKS * LAYER_COUNT * MICRO_ITEM_COUNT // ROWS)
    picked_specialist_ids_turns = jax.random.permutation(jax.random.fold_in(keys[6], 3), TICKS * LAYER_COUNT * MICRO_ITEM_COUNT // ROWS)
    picked_specialist_ids = jax.vmap(lambda own, number: deal_out(jax.random.fold_in(keys[6], 2), own, number, ROWS, EXPERTS, TOPK, CAP, 2))(picked_specialist_ids_keys, picked_specialist_ids_turns).reshape((TICKS, LAYER_COUNT, MICRO_ITEM_COUNT, TOPK))
    dispatcher_probability_values = jnp.clip(jnp.exp(math.log(1.0) - 2.3025851 * jax.random.uniform(keys[7], (TICKS, LAYER_COUNT, MICRO_ITEM_COUNT, TOPK), jnp.float32) ** shard_levels(keys[7], (TICKS, LAYER_COUNT, MICRO_ITEM_COUNT, TOPK), ((1, 16), (2, 32)), -0.2, 0.2)), 0.1, 1.0)
    return dict(pending_activations=pending_activations, incoming_microbatches=incoming_microbatches, layer_rescale_factor=layer_rescale_factor, gating_projection_matrix=gating_projection_matrix, widening_projection_matrix=widening_projection_matrix, output_projection_matrix=output_projection_matrix, picked_specialist_ids=picked_specialist_ids, dispatcher_probability_values=dispatcher_probability_values)


def section_layer(inputs, gain_row, gate_w, up_w, down_w, chosen, scores):
    float_rows = inputs.astype(jnp.float32)
    variance = lax.optimization_barrier(jnp.mean(float_rows * float_rows, axis=-1, keepdims=True))
    normed = (float_rows * lax.rsqrt(variance + 1e-06) * gain_row).astype(jnp.bfloat16)
    weights = scores
    flat_ids = chosen.reshape(N_EP, ROWS * TOPK).astype(jnp.int32)
    expert_grid = jnp.arange(EXPERTS, dtype=jnp.int32)
    hits = (flat_ids[:, :, None] == expert_grid[None, None, :]).astype(jnp.int32)
    before = jnp.cumsum(hits, axis=1) - hits
    position = lax.optimization_barrier(jnp.sum(before * hits, axis=2))
    source_grid = jnp.arange(N_EP, dtype=jnp.int32)[:, None]
    slot_index = (flat_ids * (N_EP * CAP) + source_grid * CAP + position).reshape(-1).astype(jnp.int32)
    token_of = (jnp.arange(N_EP * ROWS * TOPK, dtype=jnp.int32) // TOPK).astype(jnp.int32)
    total_slots = EXPERTS * N_EP * CAP
    source_row = jnp.zeros((total_slots,), jnp.int32).at[slot_index].set(token_of)
    filled = jnp.zeros((total_slots,), jnp.float32).at[slot_index].set(1.0)
    rows_in = (normed[source_row].astype(jnp.float32) * filled[:, None]).astype(jnp.bfloat16)
    rows_in = rows_in.reshape(EXPERTS, N_EP * CAP, HIDDEN_SPAN)
    gate_stack = jnp.transpose(gate_w.reshape(HIDDEN_SPAN, EXPERTS, FF), (1, 0, 2))
    up_stack = jnp.transpose(up_w.reshape(HIDDEN_SPAN, EXPERTS, FF), (1, 0, 2))
    down_stack = down_w.reshape(EXPERTS, GROUP, FF // GROUP, HIDDEN_SPAN)

    def one_expert(packed):
        rows_e, gate_e, up_e, down_e = packed
        gate_val = jnp.dot(rows_e, gate_e, preferred_element_type=jnp.float32)
        up_val = jnp.dot(rows_e, up_e, preferred_element_type=jnp.float32)
        active = (jax.nn.silu(gate_val) * up_val).astype(jnp.bfloat16)
        active = active.reshape(active.shape[0], GROUP, FF // GROUP)
        parts = jnp.einsum('tgf,gfd->gtd', active.astype(jnp.float32), down_e.astype(jnp.float32)).astype(jnp.bfloat16)
        return lax.optimization_barrier(jnp.sum(parts.astype(jnp.float32), axis=0))
    expert_outs = lax.map(one_expert, (rows_in, gate_stack, up_stack, down_stack))
    expert_outs = expert_outs.reshape(total_slots, HIDDEN_SPAN)
    picked = expert_outs[slot_index].reshape(N_EP * ROWS, TOPK, HIDDEN_SPAN)
    combined = lax.optimization_barrier(jnp.sum(weights[:, :, None] * picked, axis=1))
    return (float_rows + combined).astype(jnp.bfloat16)

def reference(pending_activations, incoming_microbatches, layer_rescale_factor, gating_projection_matrix, widening_projection_matrix, output_projection_matrix, picked_specialist_ids, dispatcher_probability_values):
    present_activation_list = pending_activations
    results = []
    for tick_index in range(TICKS):
        produced = []
        for section_index in range(LAYER_COUNT):
            produced.append(section_layer(present_activation_list[section_index], layer_rescale_factor[section_index], gating_projection_matrix[section_index], widening_projection_matrix[section_index], output_projection_matrix[section_index], picked_specialist_ids[tick_index, section_index], dispatcher_probability_values[tick_index, section_index]))
        produced = jnp.stack(produced)
        results.append(produced)
        if tick_index + 1 < TICKS:
            present_activation_list = jnp.concatenate([incoming_microbatches[tick_index][None], produced[:-1]], axis=0)
    return jnp.stack(results)
```

```python
import jax
import jax.numpy as jnp
from jax import lax
from jax.sharding import Mesh, PartitionSpec as P

GROUP = 8


def slots_of(chosen, slot_count, experts):
    hits = (chosen[:, None] == jnp.arange(experts, dtype=jnp.int32)[None, :]).astype(jnp.int32)
    before = jnp.cumsum(hits, axis=0) - hits
    return chosen * slot_count + jnp.sum(before * hits, axis=1)


def section_layer(inputs, gain_row, gate_w, up_w, down_w, chosen, scores):
    row_count, width = inputs.shape
    experts = lax.axis_size("x")
    ring = lax.axis_size("y")
    slot_count = 17
    float_rows = inputs.astype(jnp.float32)
    variance = jnp.mean(float_rows * float_rows, axis=-1, keepdims=True)
    normed = (float_rows * lax.rsqrt(variance + 1e-06) * gain_row).astype(jnp.bfloat16)
    slot_ids = slots_of(chosen[:, 0], slot_count, experts)
    slot_grid = jnp.arange(experts * slot_count, dtype=jnp.int32)
    picker = (slot_grid[:, None] == slot_ids[None, :]).astype(jnp.bfloat16)
    packed = jnp.dot(picker, normed, preferred_element_type=jnp.float32).astype(jnp.bfloat16)
    sent = packed.reshape(experts, slot_count, width)
    mine = lax.all_to_all(sent, "x", split_axis=0, concat_axis=0, tiled=True)
    mine = mine.reshape(experts * slot_count, width)
    held = experts * slot_count
    padded = -(-held // 8) * 8
    mine = jnp.pad(mine, ((0, padded - held), (0, 0)))
    rows = lax.all_gather(mine, "y", axis=0, tiled=True)
    gate_val = jnp.dot(rows, gate_w, preferred_element_type=jnp.float32)
    up_val = jnp.dot(rows, up_w, preferred_element_type=jnp.float32)
    active = (jax.nn.silu(gate_val) * up_val).astype(jnp.bfloat16)
    partial = jnp.dot(active, down_w, preferred_element_type=jnp.float32).astype(jnp.bfloat16)
    summed = lax.psum_scatter(partial, "y", scatter_dimension=0, tiled=True)
    back = summed[:held].reshape(experts, slot_count, width)
    back = lax.all_to_all(back, "x", split_axis=0, concat_axis=0, tiled=True)
    back = back.reshape(held, width)
    unpick = (slot_ids[:, None] == slot_grid[None, :]).astype(jnp.bfloat16)
    combined = scores * jnp.dot(unpick, back, preferred_element_type=jnp.float32)
    return (float_rows + combined).astype(jnp.bfloat16)


def local(pending, incoming, gain, gate_w, up_w, down_w, chosen, scores):
    tick_total = chosen.shape[0]
    first_section = lax.axis_index("pp") == 0
    count = lax.axis_size("pp")
    rows = pending[0]
    outputs = []
    for tick in range(tick_total):
        produced = section_layer(
            rows, gain[0], gate_w[0], up_w[0], down_w[0], chosen[tick, 0], scores[tick, 0]
        )
        outputs.append(produced)
        if tick + 1 < tick_total:
            passed = lax.ppermute(produced, "pp", [(i, i + 1) for i in range(count - 1)])
            rows = jnp.where(first_section, incoming[tick], passed)
    return jnp.stack(outputs)[:, None]


def solution(mesh):
    fine = Mesh(mesh.devices.reshape(mesh.shape["pp"], -1, GROUP), ("pp", "x", "y"))
    ep = ("x", "y")
    in_specs = (
        P("pp", ep, None),
        P(None, ep, None),
        P("pp", None),
        P("pp", None, ep),
        P("pp", None, ep),
        P("pp", ep, None),
        P(None, "pp", ep, None),
        P(None, "pp", ep, None),
    )
    out_specs = P(None, "pp", ep, None)
    return jax.shard_map(local, mesh=fine, in_specs=in_specs, out_specs=out_specs, check_vma=False)
```

```python
import functools

import jax
import jax.numpy as jnp
from jax import lax
from jax.experimental import pallas as pl
from jax.experimental.pallas import tpu as pltpu
from jax.sharding import Mesh, PartitionSpec as P

GROUP = 8
SLOTS = 17


def shift(value, steps):
    size = lax.axis_size("y")
    return lax.ppermute(value, "y", [(i, (i + steps) % size) for i in range(size)])


def expert_kernel(count, *refs):
    halves, (gate_ref, up_ref, down_ref) = refs[: 2 * count], refs[2 * count : 2 * count + 3]
    outs, (rows, active) = refs[2 * count + 3 : 4 * count + 3], refs[4 * count + 3 :]
    tall, half = halves[0].shape
    for i in range(count):
        rows[i * tall : (i + 1) * tall, :half] = halves[2 * i][...]
        rows[i * tall : (i + 1) * tall, half:] = halves[2 * i + 1][...]
    gate_val = jnp.dot(rows[...], gate_ref[...], preferred_element_type=jnp.float32)
    up_val = jnp.dot(rows[...], up_ref[...], preferred_element_type=jnp.float32)
    active[...] = (gate_val / (1.0 + jnp.exp(-gate_val)) * up_val).astype(jnp.bfloat16)
    tile = half // 2
    for j in range(4):
        part = jnp.dot(
            active[...],
            down_ref[:, j * tile : (j + 1) * tile],
            preferred_element_type=jnp.float32,
        ).astype(jnp.bfloat16)
        for i in range(count):
            outs[2 * i + j // 2][:, (j % 2) * tile : (j % 2 + 1) * tile] = part[
                i * tall : (i + 1) * tall
            ]


def expert_blocks(blocks, gate_w, up_w, down_w):
    count = len(blocks)
    tall, half = blocks[0][0].shape
    hidden = gate_w.shape[1]
    total = count * tall
    outs = pl.pallas_call(
        functools.partial(expert_kernel, count),
        out_shape=[jax.ShapeDtypeStruct((tall, half), jnp.bfloat16)] * (2 * count),
        in_specs=[pl.BlockSpec(memory_space=pltpu.VMEM)] * (2 * count + 3),
        out_specs=[pl.BlockSpec(memory_space=pltpu.VMEM)] * (2 * count),
        scratch_shapes=[
            pltpu.VMEM((total, 2 * half), jnp.bfloat16),
            pltpu.VMEM((total, hidden), jnp.bfloat16),
        ],
        cost_estimate=pl.CostEstimate(
            flops=12 * total * half * hidden,
            bytes_accessed=8 * total * half + 12 * half * hidden,
            transcendentals=total * hidden,
        ),
    )(*[h for block in blocks for h in block], gate_w, up_w, down_w)
    return [(outs[2 * i], outs[2 * i + 1]) for i in range(count)]


def plus(a, b):
    return (a.astype(jnp.float32) + b.astype(jnp.float32)).astype(jnp.bfloat16)


def ring_experts(block, gate_w, up_w, down_w):
    half = block.shape[1] // 2
    own = (block[:, :half], block[:, half:])
    ra, rb, la, lb = [own[0]], [own[1]], [own[0]], [own[1]]
    for s in range(1, 4):
        ra.append(shift(ra[-1], 1))
        lb.append(shift(lb[-1], -1))
        rb.append(shift(rb[-1], 1))
        la.append(shift(la[-1], -1))
    far = (shift(ra[-1], 1), shift(lb[-1], -1))
    near = [own] + [b for s in (1, 2, 3) for b in ((ra[s], rb[s]), (la[s], lb[s]))]
    done = expert_blocks(near, gate_w, up_w, down_w)
    left = [None] + [done[2 * s - 1] for s in (1, 2, 3)]
    right = [None] + [done[2 * s] for s in (1, 2, 3)]
    (opposite,) = expert_blocks([far], gate_w, up_w, down_w)
    rb_sum, la_sum = shift(right[3][1], 1), shift(left[3][0], -1)
    ra_sum, lb_sum = shift(opposite[0], 1), shift(opposite[1], -1)
    for s in (3, 2, 1):
        ra_sum = shift(plus(ra_sum, right[s][0]), 1)
        lb_sum = shift(plus(lb_sum, left[s][1]), -1)
        if s < 3:
            rb_sum = shift(plus(rb_sum, right[s][1]), 1)
            la_sum = shift(plus(la_sum, left[s][0]), -1)
    wide = lambda v: v.astype(jnp.float32)
    first = wide(done[0][0]) + wide(ra_sum) + wide(la_sum)
    second = wide(done[0][1]) + wide(rb_sum) + wide(lb_sum)
    return jnp.concatenate([first, second], axis=1).astype(jnp.bfloat16)


def slots_of(chosen, experts):
    hits = (chosen[:, None] == jnp.arange(experts, dtype=jnp.int32)[None, :]).astype(jnp.int32)
    before = jnp.cumsum(hits, axis=0) - hits
    return chosen * SLOTS + jnp.sum(before * hits, axis=1)


def section_layer(inputs, gain_row, gate_w, up_w, down_w, chosen, scores):
    width = inputs.shape[1]
    experts = lax.axis_size("x")
    float_rows = inputs.astype(jnp.float32)
    variance = jnp.mean(float_rows * float_rows, axis=-1, keepdims=True)
    normed = (float_rows * lax.rsqrt(variance + 1e-06) * gain_row).astype(jnp.bfloat16)
    slot_ids = slots_of(chosen[:, 0], experts)
    held = experts * SLOTS
    slot_grid = jnp.arange(held, dtype=jnp.int32)
    picker = (slot_grid[:, None] == slot_ids[None, :]).astype(jnp.bfloat16)
    packed = jnp.dot(picker, normed, preferred_element_type=jnp.float32).astype(jnp.bfloat16)
    mine = lax.all_to_all(
        packed.reshape(experts, SLOTS, width), "x", split_axis=0, concat_axis=0, tiled=True
    )
    padded = -(-held // 8) * 8
    mine = jnp.pad(mine.reshape(held, width), ((0, padded - held), (0, 0)))
    summed = ring_experts(mine, gate_w, up_w, down_w)
    back = summed[:held].reshape(experts, SLOTS, width)
    back = lax.all_to_all(back, "x", split_axis=0, concat_axis=0, tiled=True)
    back = back.reshape(held, width)
    unpick = (slot_ids[:, None] == slot_grid[None, :]).astype(jnp.bfloat16)
    combined = scores * jnp.dot(unpick, back, preferred_element_type=jnp.float32)
    return (float_rows + combined).astype(jnp.bfloat16)


def local(pending, incoming, gain, gate_w, up_w, down_w, chosen, scores):
    tick_total = chosen.shape[0]
    first_section = lax.axis_index("pp") == 0
    count = lax.axis_size("pp")
    rows = pending[0]
    outputs = []
    for tick in range(tick_total):
        produced = section_layer(
            rows, gain[0], gate_w[0], up_w[0], down_w[0], chosen[tick, 0], scores[tick, 0]
        )
        outputs.append(produced)
        if tick + 1 < tick_total:
            passed = lax.ppermute(produced, "pp", [(i, i + 1) for i in range(count - 1)])
            rows = jnp.where(first_section, incoming[tick], passed)
    return jnp.stack(outputs)[:, None]


def solution(mesh):
    fine = Mesh(mesh.devices.reshape(mesh.shape["pp"], -1, GROUP), ("pp", "x", "y"))
    ep = ("x", "y")
    in_specs = (
        P("pp", ep, None),
        P(None, ep, None),
        P("pp", None),
        P("pp", None, ep),
        P("pp", None, ep),
        P("pp", ep, None),
        P(None, "pp", ep, None),
        P(None, "pp", ep, None),
    )
    out_specs = P(None, "pp", ep, None)
    return jax.shard_map(local, mesh=fine, in_specs=in_specs, out_specs=out_specs, check_vma=False)
```

```python
import functools

import jax
import jax.numpy as jnp
from jax import lax
from jax.experimental import pallas as pl
from jax.experimental.pallas import tpu as pltpu
from jax.sharding import Mesh, PartitionSpec as P

GROUP = 8
SLOTS = 17


def shift(value, steps):
    size = lax.axis_size("y")
    return lax.ppermute(value, "y", [(i, (i + steps) % size) for i in range(size)])


def expert_kernel(spans_in, spans_out, *refs):
    n_in, n_out = sum(spans_in), sum(spans_out)
    pieces, (gate_ref, up_ref, down_ref) = refs[:n_in], refs[n_in : n_in + 3]
    outs, (rows, both, active) = refs[n_in + 3 : n_in + 3 + n_out], refs[n_in + 3 + n_out :]
    tall, width = pieces[0].shape[0], rows.shape[1]
    hidden = gate_ref.shape[1]
    at = 0
    for i, span in enumerate(spans_in):
        wide = width // span
        for k in range(span):
            rows[i * tall : (i + 1) * tall, k * wide : (k + 1) * wide] = pieces[at][...]
            at += 1
    both[:, :hidden] = gate_ref[...]
    both[:, hidden:] = up_ref[...]
    mixed = jnp.dot(rows[...], both[...], preferred_element_type=jnp.float32)
    gate_val, up_val = mixed[:, :hidden], mixed[:, hidden:]
    active[...] = (gate_val / (1.0 + jnp.exp(-gate_val)) * up_val).astype(jnp.bfloat16)
    tiles = 4
    tile = width // tiles
    for j in range(tiles):
        part = jnp.dot(
            active[...],
            down_ref[:, j * tile : (j + 1) * tile],
            preferred_element_type=jnp.float32,
        ).astype(jnp.bfloat16)
        at = 0
        for i, span in enumerate(spans_out):
            per = tiles // span
            cols = slice((j % per) * tile, (j % per + 1) * tile)
            outs[at + j // per][:, cols] = part[i * tall : (i + 1) * tall]
            at += span


def expert_blocks(blocks, spans_out, gate_w, up_w, down_w):
    spans_in = tuple(len(block) for block in blocks)
    tall = blocks[0][0].shape[0]
    width, hidden = gate_w.shape
    total = len(blocks) * tall
    shapes = [(tall, width // span) for span in spans_out for _ in range(span)]
    outs = pl.pallas_call(
        functools.partial(expert_kernel, spans_in, spans_out),
        out_shape=[pltpu.VMEM(shape, jnp.bfloat16) for shape in shapes],
        in_specs=[pl.BlockSpec(memory_space=pltpu.VMEM)] * (sum(spans_in) + 3),
        out_specs=[pl.BlockSpec(memory_space=pltpu.VMEM)] * len(shapes),
        scratch_shapes=[
            pltpu.VMEM((total, width), jnp.bfloat16),
            pltpu.VMEM((width, 2 * hidden), jnp.bfloat16),
            pltpu.VMEM((total, hidden), jnp.bfloat16),
        ],
        compiler_params=pltpu.CompilerParams(vmem_limit_bytes=24 * 2**20),
        cost_estimate=pl.CostEstimate(
            flops=6 * total * width * hidden,
            bytes_accessed=4 * total * width + 6 * width * hidden,
            transcendentals=total * hidden,
        ),
    )(
        *[pltpu.with_memory_space_constraint(p, pltpu.VMEM) for block in blocks for p in block],
        gate_w,
        up_w,
        down_w,
    )
    result, at = [], 0
    for span in spans_out:
        result.append(tuple(outs[at : at + span]))
        at += span
    return result


def plus(a, b):
    return (a.astype(jnp.float32) + b.astype(jnp.float32)).astype(jnp.bfloat16)


def ring_experts(block, gate_w, up_w, down_w):
    half = block.shape[1] // 2
    ra, rb, whole = [block[:, :half]], [block[:, half:]], [block]
    for s in range(1, 4):
        ra.append(shift(ra[-1], 1))
        rb.append(shift(rb[-1], 1))
        whole.append(shift(whole[-1], -1))
    far = (shift(ra[-1], 1), shift(rb[-1], 1))
    near = [(block,)] + [b for s in (1, 2, 3) for b in ((ra[s], rb[s]), (whole[s],))]
    done = expert_blocks(near, (1, 1, 2, 1, 2, 1, 2), gate_w, up_w, down_w)
    left = [None] + [done[2 * s - 1][0] for s in (1, 2, 3)]
    right = [None] + [done[2 * s] for s in (1, 2, 3)]
    (opposite,) = expert_blocks([far], (2,), gate_w, up_w, down_w)
    a_sum, b_sum = shift(opposite[0], 1), shift(opposite[1], 1)
    l_sum = shift(left[3], -1)
    for s in (3, 2, 1):
        a_sum = shift(plus(a_sum, right[s][0]), 1)
        b_sum = shift(plus(b_sum, right[s][1]), 1)
        if s < 3:
            l_sum = shift(plus(l_sum, left[s]), -1)
    wide = lambda v: v.astype(jnp.float32)
    sums = jnp.concatenate([a_sum, b_sum], axis=1)
    return (wide(done[0][0]) + wide(l_sum) + wide(sums)).astype(jnp.bfloat16)


def slots_of(chosen, experts):
    hits = (chosen[:, None] == jnp.arange(experts, dtype=jnp.int32)[None, :]).astype(jnp.int32)
    before = jnp.cumsum(hits, axis=0) - hits
    return chosen * SLOTS + jnp.sum(before * hits, axis=1)


def section_layer(inputs, gain_row, gate_w, up_w, down_w, chosen, scores):
    width = inputs.shape[1]
    experts = lax.axis_size("x")
    float_rows = inputs.astype(jnp.float32)
    variance = jnp.mean(float_rows * float_rows, axis=-1, keepdims=True)
    normed = (float_rows * lax.rsqrt(variance + 1e-06) * gain_row).astype(jnp.bfloat16)
    slot_ids = slots_of(chosen[:, 0], experts)
    held = experts * SLOTS
    slot_grid = jnp.arange(held, dtype=jnp.int32)
    picker = (slot_grid[:, None] == slot_ids[None, :]).astype(jnp.bfloat16)
    packed = jnp.dot(picker, normed, preferred_element_type=jnp.float32).astype(jnp.bfloat16)
    mine = lax.all_to_all(
        packed.reshape(experts, SLOTS, width), "x", split_axis=0, concat_axis=0, tiled=True
    )
    padded = -(-held // 8) * 8
    mine = jnp.pad(mine.reshape(held, width), ((0, padded - held), (0, 0)))
    summed = ring_experts(mine, gate_w, up_w, down_w)
    back = summed[:held].reshape(experts, SLOTS, width)
    back = lax.all_to_all(back, "x", split_axis=0, concat_axis=0, tiled=True)
    back = back.reshape(held, width)
    unpick = (slot_ids[:, None] == slot_grid[None, :]).astype(jnp.bfloat16)
    combined = scores * jnp.dot(unpick, back, preferred_element_type=jnp.float32)
    return (float_rows + combined).astype(jnp.bfloat16)


def local(pending, incoming, gain, gate_w, up_w, down_w, chosen, scores):
    tick_total = chosen.shape[0]
    first_section = lax.axis_index("pp") == 0
    count = lax.axis_size("pp")
    rows = pending[0]
    outputs = []
    for tick in range(tick_total):
        produced = section_layer(
            rows, gain[0], gate_w[0], up_w[0], down_w[0], chosen[tick, 0], scores[tick, 0]
        )
        outputs.append(produced)
        if tick + 1 < tick_total:
            passed = lax.ppermute(produced, "pp", [(i, i + 1) for i in range(count - 1)])
            rows = jnp.where(first_section, incoming[tick], passed)
    return jnp.stack(outputs)[:, None]


def solution(mesh):
    fine = Mesh(mesh.devices.reshape(mesh.shape["pp"], -1, GROUP), ("pp", "x", "y"))
    ep = ("x", "y")
    in_specs = (
        P("pp", ep, None),
        P(None, ep, None),
        P("pp", None),
        P("pp", None, ep),
        P("pp", None, ep),
        P("pp", ep, None),
        P(None, "pp", ep, None),
        P(None, "pp", ep, None),
    )
    out_specs = P(None, "pp", ep, None)
    return jax.shard_map(local, mesh=fine, in_specs=in_specs, out_specs=out_specs, check_vma=False)
```

```python
import functools

import jax
import jax.numpy as jnp
from jax import lax
from jax.experimental import pallas as pl
from jax.experimental.pallas import tpu as pltpu
from jax.sharding import Mesh, PartitionSpec as P

GROUP = 8
RING_SLOTS = 8
BULK_SLOTS = 9


def shift(value, steps):
    size = lax.axis_size("y")
    return lax.ppermute(value, "y", [(i, (i + steps) % size) for i in range(size)])


def expert_kernel(spans_in, spans_out, *refs):
    n_in, n_out = sum(spans_in), sum(spans_out)
    pieces, (gate_ref, up_ref, down_ref) = refs[:n_in], refs[n_in : n_in + 3]
    outs, (rows, both, active) = refs[n_in + 3 : n_in + 3 + n_out], refs[n_in + 3 + n_out :]
    tall, width = pieces[0].shape[0], rows.shape[1]
    hidden = gate_ref.shape[1]
    at = 0
    for i, span in enumerate(spans_in):
        wide = width // span
        for k in range(span):
            rows[i * tall : (i + 1) * tall, k * wide : (k + 1) * wide] = pieces[at][...]
            at += 1
    both[:, :hidden] = gate_ref[...]
    both[:, hidden:] = up_ref[...]
    mixed = jnp.dot(rows[...], both[...], preferred_element_type=jnp.float32)
    gate_val, up_val = mixed[:, :hidden], mixed[:, hidden:]
    active[...] = (gate_val / (1.0 + jnp.exp(-gate_val)) * up_val).astype(jnp.bfloat16)
    tiles = 4
    tile = width // tiles
    for j in range(tiles):
        part = jnp.dot(
            active[...],
            down_ref[:, j * tile : (j + 1) * tile],
            preferred_element_type=jnp.float32,
        ).astype(jnp.bfloat16)
        at = 0
        for i, span in enumerate(spans_out):
            per = tiles // span
            cols = slice((j % per) * tile, (j % per + 1) * tile)
            outs[at + j // per][:, cols] = part[i * tall : (i + 1) * tall]
            at += span


def expert_blocks(blocks, gate_w, up_w, down_w):
    spans = tuple(len(block) for block in blocks)
    tall = blocks[0][0].shape[0]
    width, hidden = gate_w.shape
    total = len(blocks) * tall
    pieces = [p for block in blocks for p in block]
    shapes = [jax.ShapeDtypeStruct((tall, width // span), jnp.bfloat16) for span in spans for _ in range(span)]
    outs = pl.pallas_call(
        functools.partial(expert_kernel, spans, spans),
        out_shape=shapes,
        in_specs=[pl.BlockSpec(memory_space=pltpu.VMEM)] * (len(pieces) + 3),
        out_specs=[pl.BlockSpec(memory_space=pltpu.VMEM)] * len(shapes),
        scratch_shapes=[
            pltpu.VMEM((total, width), jnp.bfloat16),
            pltpu.VMEM((width, 2 * hidden), jnp.bfloat16),
            pltpu.VMEM((total, hidden), jnp.bfloat16),
        ],
        cost_estimate=pl.CostEstimate(
            flops=6 * total * width * hidden,
            bytes_accessed=4 * total * width + 6 * width * hidden,
            transcendentals=total * hidden,
        ),
    )(*pieces, gate_w, up_w, down_w)
    result, at = [], 0
    for span in spans:
        result.append(tuple(outs[at : at + span]))
        at += span
    return result


def plus(a, b):
    return (a.astype(jnp.float32) + b.astype(jnp.float32)).astype(jnp.bfloat16)


def wide(value):
    return value.astype(jnp.float32)


def exchange(packed, slots):
    experts = lax.axis_size("x")
    blocks = packed.reshape(experts, slots, packed.shape[1])
    moved = lax.all_to_all(blocks, "x", split_axis=0, concat_axis=0, tiled=True)
    return moved.reshape(packed.shape)


def experts_of(ring_rows, bulk_rows, gate_w, up_w, down_w):
    weights = (gate_w, up_w, down_w)
    tie = lax.optimization_barrier
    bulk_held = bulk_rows.shape[0]
    bulk_tall = -(-bulk_held // 8) * 8
    bulk = exchange(bulk_rows, BULK_SLOTS)
    ring_rows, bulk = tie((ring_rows, bulk))
    bulk = jnp.pad(bulk, ((0, bulk_tall - bulk_held), (0, 0)))
    bulk_all = lax.all_gather(bulk, "y", axis=0, tiled=True)
    block = exchange(ring_rows, RING_SLOTS)
    from_left, from_right = [block], [block]
    for s in range(1, 4):
        pair = tie((shift(from_left[-1], 1), shift(from_right[-1], -1)))
        from_left.append(pair[0])
        from_right.append(pair[1])
    far = shift(from_left[-1], 1)
    bulk_all, far = tie((bulk_all, far))
    ((bulk_part,),) = expert_blocks([(bulk_all,)], *weights)
    bulk_sum = lax.psum_scatter(bulk_part, "y", scatter_dimension=0, tiled=True)
    far, bulk_part = tie((far, bulk_part))
    done = expert_blocks(
        [(v,) for v in [block] + from_left[1:] + from_right[1:] + [far]], *weights
    )
    own, left, right, opposite = done[0], done[1:4], done[4:7], done[7]
    to_right, to_left = tie((shift(opposite[0], 1), shift(left[2][0], -1)))
    for s in (2, 1):
        to_right = plus(to_right, right[s][0])
        to_left = plus(to_left, left[s - 1][0])
        to_right, to_left = tie((shift(to_right, 1), shift(to_left, -1)))
    to_right = shift(plus(to_right, right[0][0]), 1)
    ring_sum = (wide(own[0]) + wide(to_left) + wide(to_right)).astype(jnp.bfloat16)
    ring_back = exchange(ring_sum, RING_SLOTS)
    bulk_sum, ring_back = tie((bulk_sum, ring_back))
    return ring_back, exchange(bulk_sum[:bulk_held], BULK_SLOTS)


def section_layer(inputs, gain_row, gate_w, up_w, down_w, chosen, scores):
    experts = lax.axis_size("x")
    float_rows = wide(inputs)
    variance = jnp.mean(float_rows * float_rows, axis=-1, keepdims=True)
    normed = (float_rows * lax.rsqrt(variance + 1e-06) * gain_row).astype(jnp.bfloat16)
    chosen = chosen[:, 0]
    hits = (chosen[:, None] == jnp.arange(experts, dtype=jnp.int32)[None, :]).astype(jnp.int32)
    place = jnp.sum((jnp.cumsum(hits, axis=0) - hits) * hits, axis=1)
    first = place < RING_SLOTS
    ring_slot = jnp.where(first, chosen * RING_SLOTS + place, -1)
    bulk_slot = jnp.where(first, -1, chosen * BULK_SLOTS + place - RING_SLOTS)

    def pick(slot, count):
        return (jnp.arange(count, dtype=jnp.int32)[:, None] == slot[None, :]).astype(jnp.bfloat16)

    def pack(slot, count):
        return jnp.dot(
            pick(slot, count), normed, preferred_element_type=jnp.float32
        ).astype(jnp.bfloat16)

    def unpack(slot, values):
        return jnp.dot(
            pick(slot, values.shape[0]).T, values, preferred_element_type=jnp.float32
        )

    ring_back, bulk_back = experts_of(
        pack(ring_slot, experts * RING_SLOTS),
        pack(bulk_slot, experts * BULK_SLOTS),
        gate_w,
        up_w,
        down_w,
    )
    combined = unpack(ring_slot, ring_back) + unpack(bulk_slot, bulk_back)
    return (float_rows + scores * combined).astype(jnp.bfloat16)


def local(pending, incoming, gain, gate_w, up_w, down_w, chosen, scores):
    tick_total = chosen.shape[0]
    first_section = lax.axis_index("pp") == 0
    count = lax.axis_size("pp")
    rows = pending[0]
    outputs = []
    for tick in range(tick_total):
        produced = section_layer(
            rows, gain[0], gate_w[0], up_w[0], down_w[0], chosen[tick, 0], scores[tick, 0]
        )
        outputs.append(produced)
        if tick + 1 < tick_total:
            passed = lax.ppermute(produced, "pp", [(i, i + 1) for i in range(count - 1)])
            rows = jnp.where(first_section, incoming[tick], passed)
    return jnp.stack(outputs)[:, None]


def solution(mesh):
    fine = Mesh(mesh.devices.reshape(mesh.shape["pp"], -1, GROUP), ("pp", "x", "y"))
    ep = ("x", "y")
    in_specs = (
        P("pp", ep, None),
        P(None, ep, None),
        P("pp", None),
        P("pp", None, ep),
        P("pp", None, ep),
        P("pp", ep, None),
        P(None, "pp", ep, None),
        P(None, "pp", ep, None),
    )
    out_specs = P(None, "pp", ep, None)
    return jax.shard_map(local, mesh=fine, in_specs=in_specs, out_specs=out_specs, check_vma=False)
```

```python
import jax
import jax.numpy as jnp
from jax import lax
from jax.experimental import pallas as pl
from jax.experimental.pallas import tpu as pltpu
from jax.sharding import Mesh, PartitionSpec as P

GROUP = 8
SLOTS = 17
SUM_ROWS = 71


def expert_kernel(rows_ref, gate_ref, up_ref, down_ref, out_ref, rows, both, active, packed):
    tall = rows_ref.shape[0] // GROUP
    short = out_ref.shape[0] // GROUP
    hidden = gate_ref.shape[1]
    rows[...] = rows_ref[...]
    both[:, :hidden] = gate_ref[...]
    both[:, hidden:] = up_ref[...]
    mixed = jnp.dot(rows[...], both[...], preferred_element_type=jnp.float32)
    gate_val, up_val = mixed[:, :hidden], mixed[:, hidden:]
    active[...] = gate_val / (1.0 + jnp.exp(-gate_val)) * up_val
    for i in range(GROUP):
        packed[i * short : (i + 1) * short, :] = active[i * tall : i * tall + short, :]
    acts = packed[...].astype(jnp.bfloat16)
    tile = down_ref.shape[1] // 4
    for j in range(4):
        cols = slice(j * tile, (j + 1) * tile)
        out_ref[:, cols] = jnp.dot(
            acts, down_ref[:, cols], preferred_element_type=jnp.float32
        ).astype(jnp.bfloat16)


def expert_parts(rows, gate_w, up_w, down_w):
    total, width = rows.shape
    hidden = gate_w.shape[1]
    return pl.pallas_call(
        expert_kernel,
        out_shape=jax.ShapeDtypeStruct((GROUP * SUM_ROWS, width), jnp.bfloat16),
        in_specs=[pl.BlockSpec(memory_space=pltpu.VMEM)] * 4,
        out_specs=pl.BlockSpec(memory_space=pltpu.VMEM),
        scratch_shapes=[
            pltpu.VMEM((total, width), jnp.bfloat16),
            pltpu.VMEM((width, 2 * hidden), jnp.bfloat16),
            pltpu.VMEM((total, hidden), jnp.float32),
            pltpu.VMEM((GROUP * SUM_ROWS, hidden), jnp.float32),
        ],
        compiler_params=pltpu.CompilerParams(vmem_limit_bytes=32 * 2**20),
        cost_estimate=pl.CostEstimate(
            flops=6 * total * width * hidden,
            bytes_accessed=4 * total * width + 6 * width * hidden,
            transcendentals=total * hidden,
        ),
    )(rows, gate_w, up_w, down_w)


def wide(value):
    return value.astype(jnp.float32)


def exchange(packed):
    experts = lax.axis_size("x")
    blocks = packed.reshape(experts, SLOTS, packed.shape[1])
    moved = lax.all_to_all(blocks, "x", split_axis=0, concat_axis=0, tiled=True)
    return moved.reshape(packed.shape)


def experts_of(packed, gate_w, up_w, down_w):
    held = packed.shape[0]
    tall = -(-held // 8) * 8
    mine = jnp.pad(exchange(packed), ((0, tall - held), (0, 0)))
    rows = lax.all_gather(mine.astype(jnp.float16), "y", axis=0, tiled=True)
    parts = expert_parts(rows.astype(jnp.bfloat16), gate_w, up_w, down_w)
    summed = lax.psum_scatter(parts, "y", scatter_dimension=0, tiled=True)
    summed = lax.optimization_barrier(summed)
    return exchange(summed[:held])


def section_layer(inputs, gain_row, gate_w, up_w, down_w, chosen, scores):
    experts = lax.axis_size("x")
    float_rows = wide(inputs)
    variance = jnp.mean(float_rows * float_rows, axis=-1, keepdims=True)
    normed = (float_rows * lax.rsqrt(variance + 1e-06) * gain_row).astype(jnp.bfloat16)
    chosen = chosen[:, 0]
    hits = (chosen[:, None] == jnp.arange(experts, dtype=jnp.int32)[None, :]).astype(jnp.int32)
    place = jnp.sum((jnp.cumsum(hits, axis=0) - hits) * hits, axis=1)
    slot = chosen * SLOTS + place

    count = experts * SLOTS
    pick = (jnp.arange(count, dtype=jnp.int32)[:, None] == slot[None, :]).astype(jnp.bfloat16)
    packed = jnp.dot(pick, normed, preferred_element_type=jnp.float32).astype(jnp.bfloat16)
    back = experts_of(packed, gate_w, up_w, down_w)
    combined = jnp.dot(pick.T, back, preferred_element_type=jnp.float32)
    return (float_rows + scores * combined).astype(jnp.bfloat16)


def local(pending, incoming, gain, gate_w, up_w, down_w, chosen, scores):
    tick_total = chosen.shape[0]
    first_section = lax.axis_index("pp") == 0
    count = lax.axis_size("pp")
    rows = pending[0]
    outputs = []
    for tick in range(tick_total):
        produced = section_layer(
            rows, gain[0], gate_w[0], up_w[0], down_w[0], chosen[tick, 0], scores[tick, 0]
        )
        outputs.append(produced)
        if tick + 1 < tick_total:
            passed = lax.ppermute(produced, "pp", [(i, i + 1) for i in range(count - 1)])
            rows = jnp.where(first_section, incoming[tick], passed)
    return jnp.stack(outputs)[:, None]


def solution(mesh):
    fine = Mesh(mesh.devices.reshape(mesh.shape["pp"], -1, GROUP), ("pp", "x", "y"))
    ep = ("x", "y")
    in_specs = (
        P("pp", ep, None),
        P(None, ep, None),
        P("pp", None),
        P("pp", None, ep),
        P("pp", None, ep),
        P("pp", ep, None),
        P(None, "pp", ep, None),
        P(None, "pp", ep, None),
    )
    out_specs = P(None, "pp", ep, None)
    return jax.shard_map(local, mesh=fine, in_specs=in_specs, out_specs=out_specs, check_vma=False)
```

```python
import jax
import jax.numpy as jnp
from jax import lax
from jax.experimental import pallas as pl
from jax.experimental.pallas import tpu as pltpu
from jax.sharding import Mesh, PartitionSpec as P

GROUP = 8
SLOTS = 17
LANES = 24


def shift(value, steps):
    size = lax.axis_size("y")
    return lax.ppermute(value, "y", [(i, (i + steps) % size) for i in range(size)])


def expert_kernel(me_ref, rows_ref, gate_ref, up_ref, down_ref, *refs):
    outs, (both, active, turned) = refs[:-3], refs[-3:]
    tall = rows_ref.shape[0] // GROUP
    width, hidden = gate_ref.shape
    both[:, :hidden] = gate_ref[...]
    both[:, hidden:] = up_ref[...]
    mixed = jnp.dot(rows_ref[...], both[...], preferred_element_type=jnp.float32)
    gate_val, up_val = mixed[:, :hidden], mixed[:, hidden:]
    active[...] = gate_val / (1.0 + jnp.exp(-gate_val)) * up_val
    for d in range(GROUP):
        owner = lax.rem(me_ref[0] + d, GROUP)
        block = active[pl.ds(pl.multiple_of(owner * tall, 8), tall), :]
        turned[d * tall : (d + 1) * tall, :] = block
    acts = turned[...].astype(jnp.bfloat16)
    tile = width // 4
    for j in range(4):
        part = jnp.dot(
            acts, down_ref[:, j * tile : (j + 1) * tile], preferred_element_type=jnp.float32
        ).astype(jnp.bfloat16)
        cols = slice((j % 2) * tile, (j % 2 + 1) * tile)
        for d in range(GROUP):
            outs[2 * d + j // 2][:, cols] = part[d * tall : (d + 1) * tall]


def expert_parts(rows, gate_w, up_w, down_w):
    total, width = rows.shape
    hidden = gate_w.shape[1]
    me = lax.axis_index("y").astype(jnp.int32).reshape(1)
    outs = pl.pallas_call(
        expert_kernel,
        out_shape=[pltpu.VMEM((total // GROUP, width // 2), jnp.bfloat16)] * (2 * GROUP),
        in_specs=[pl.BlockSpec(memory_space=pltpu.SMEM)]
        + [pl.BlockSpec(memory_space=pltpu.VMEM)] * 4,
        out_specs=[pl.BlockSpec(memory_space=pltpu.VMEM)] * (2 * GROUP),
        scratch_shapes=[
            pltpu.VMEM((width, 2 * hidden), jnp.bfloat16),
            pltpu.VMEM((total, hidden), jnp.float32),
            pltpu.VMEM((total, hidden), jnp.float32),
        ],
        compiler_params=pltpu.CompilerParams(vmem_limit_bytes=24 * 2**20),
        cost_estimate=pl.CostEstimate(
            flops=6 * total * width * hidden,
            bytes_accessed=4 * total * width + 6 * width * hidden,
            transcendentals=total * hidden,
        ),
    )(me, rows, gate_w, up_w, down_w)
    return [(outs[2 * d], outs[2 * d + 1]) for d in range(GROUP)]


def wide(value):
    return value.astype(jnp.float32)


def plus(a, b):
    return (a.astype(jnp.float32) + b.astype(jnp.float32)).astype(jnp.bfloat16)


def exchange(packed):
    experts = lax.axis_size("x")
    blocks = packed.reshape(experts, LANES, packed.shape[1])
    moved = lax.all_to_all(blocks, "x", split_axis=0, concat_axis=0, tiled=True)
    return moved.reshape(packed.shape)


def ring_sum(parts):
    right_a, left_b = shift(parts[4][0], 1), shift(parts[4][1], -1)
    right_b, left_a = shift(parts[3][1], 1), shift(parts[5][0], -1)
    for s in (3, 2, 1):
        right_a = shift(plus(right_a, parts[s][0]), 1)
        left_b = shift(plus(left_b, parts[GROUP - s][1]), -1)
        if s < 3:
            right_b = shift(plus(right_b, parts[s][1]), 1)
            left_a = shift(plus(left_a, parts[GROUP - s][0]), -1)
    first = wide(parts[0][0]) + wide(right_a) + wide(left_a)
    second = wide(parts[0][1]) + wide(right_b) + wide(left_b)
    return first.astype(jnp.bfloat16), second.astype(jnp.bfloat16)


def select(matrix, values):
    return jnp.dot(matrix, values, preferred_element_type=jnp.float32).astype(jnp.bfloat16)


def experts_of(packed, gate_w, up_w, down_w):
    experts = lax.axis_size("x")
    held = experts * SLOTS
    tall = -(-held // 8) * 8
    lane = jnp.arange(experts * LANES, dtype=jnp.int32)
    dense = jnp.where(lane % LANES < SLOTS, lane // LANES * SLOTS + lane % LANES, -1)
    spread = (dense[:, None] == jnp.arange(tall, dtype=jnp.int32)[None, :]).astype(jnp.bfloat16)
    mine = select(spread.T, exchange(packed))
    rows = lax.all_gather(mine.astype(jnp.float16), "y", axis=0, tiled=True)
    parts = expert_parts(rows.astype(jnp.bfloat16), gate_w, up_w, down_w)
    halves = [select(spread, half) for half in ring_sum(parts)]
    return exchange(jnp.concatenate(halves, axis=1))


def section_layer(inputs, gain_row, gate_w, up_w, down_w, chosen, scores):
    experts = lax.axis_size("x")
    float_rows = wide(inputs)
    variance = jnp.mean(float_rows * float_rows, axis=-1, keepdims=True)
    normed = (float_rows * lax.rsqrt(variance + 1e-06) * gain_row).astype(jnp.bfloat16)
    chosen = chosen[:, 0]
    hits = (chosen[:, None] == jnp.arange(experts, dtype=jnp.int32)[None, :]).astype(jnp.int32)
    place = jnp.sum((jnp.cumsum(hits, axis=0) - hits) * hits, axis=1)
    slot = chosen * LANES + place

    count = experts * LANES
    pick = (jnp.arange(count, dtype=jnp.int32)[:, None] == slot[None, :]).astype(jnp.bfloat16)
    packed = jnp.dot(pick, normed, preferred_element_type=jnp.float32).astype(jnp.bfloat16)
    back = experts_of(packed, gate_w, up_w, down_w)
    combined = jnp.dot(pick.T, back, preferred_element_type=jnp.float32)
    return (float_rows + scores * combined).astype(jnp.bfloat16)


def local(pending, incoming, gain, gate_w, up_w, down_w, chosen, scores):
    tick_total = chosen.shape[0]
    first_section = lax.axis_index("pp") == 0
    count = lax.axis_size("pp")
    rows = pending[0]
    outputs = []
    for tick in range(tick_total):
        produced = section_layer(
            rows, gain[0], gate_w[0], up_w[0], down_w[0], chosen[tick, 0], scores[tick, 0]
        )
        outputs.append(produced)
        if tick + 1 < tick_total:
            passed = lax.ppermute(produced, "pp", [(i, i + 1) for i in range(count - 1)])
            rows = jnp.where(first_section, incoming[tick], passed)
    return jnp.stack(outputs)[:, None]


def solution(mesh):
    fine = Mesh(mesh.devices.reshape(mesh.shape["pp"], -1, GROUP), ("pp", "x", "y"))
    ep = ("x", "y")
    in_specs = (
        P("pp", ep, None),
        P(None, ep, None),
        P("pp", None),
        P("pp", None, ep),
        P("pp", None, ep),
        P("pp", ep, None),
        P(None, "pp", ep, None),
        P(None, "pp", ep, None),
    )
    out_specs = P(None, "pp", ep, None)
    return jax.shard_map(local, mesh=fine, in_specs=in_specs, out_specs=out_specs, check_vma=False)
```

```python
import jax
import jax.numpy as jnp
from jax import lax
from jax.experimental import pallas as pl
from jax.experimental.pallas import tpu as pltpu
from jax.sharding import Mesh, PartitionSpec as P

GROUP = 8
SLOTS = 17
LANES = 24


def shift(value, steps):
    size = lax.axis_size("y")
    return lax.ppermute(value, "y", [(i, (i + steps) % size) for i in range(size)])


def expert_kernel(me_ref, rows_ref, gate_ref, up_ref, down_ref, *refs):
    outs, (both, active, turned) = refs[:-3], refs[-3:]
    tall = rows_ref.shape[0] // GROUP
    width, hidden = gate_ref.shape
    both[:, :hidden] = gate_ref[...]
    both[:, hidden:] = up_ref[...]
    mixed = jnp.dot(rows_ref[...], both[...], preferred_element_type=jnp.float32)
    gate_val, up_val = mixed[:, :hidden], mixed[:, hidden:]
    active[...] = gate_val / (1.0 + jnp.exp(-gate_val)) * up_val
    for d in range(GROUP):
        owner = lax.rem(me_ref[0] + d, GROUP)
        block = active[pl.ds(pl.multiple_of(owner * tall, 8), tall), :]
        turned[d * tall : (d + 1) * tall, :] = block
    acts = turned[...].astype(jnp.bfloat16)
    tile = width // 4
    for j in range(4):
        part = jnp.dot(
            acts, down_ref[:, j * tile : (j + 1) * tile], preferred_element_type=jnp.float32
        ).astype(jnp.bfloat16)
        cols = slice((j % 2) * tile, (j % 2 + 1) * tile)
        for d in range(GROUP):
            outs[2 * d + j // 2][:, cols] = part[d * tall : (d + 1) * tall]


def expert_parts(rows, gate_w, up_w, down_w):
    total, width = rows.shape
    hidden = gate_w.shape[1]
    me = lax.axis_index("y").astype(jnp.int32).reshape(1)
    outs = pl.pallas_call(
        expert_kernel,
        out_shape=[pltpu.VMEM((total // GROUP, width // 2), jnp.bfloat16)] * (2 * GROUP),
        in_specs=[pl.BlockSpec(memory_space=pltpu.SMEM)]
        + [pl.BlockSpec(memory_space=pltpu.VMEM)] * 4,
        out_specs=[pl.BlockSpec(memory_space=pltpu.VMEM)] * (2 * GROUP),
        scratch_shapes=[
            pltpu.VMEM((width, 2 * hidden), jnp.bfloat16),
            pltpu.VMEM((total, hidden), jnp.float32),
            pltpu.VMEM((total, hidden), jnp.float32),
        ],
        compiler_params=pltpu.CompilerParams(vmem_limit_bytes=24 * 2**20),
        cost_estimate=pl.CostEstimate(
            flops=6 * total * width * hidden,
            bytes_accessed=4 * total * width + 6 * width * hidden,
            transcendentals=total * hidden,
        ),
    )(me, rows, gate_w, up_w, down_w)
    return [(outs[2 * d], outs[2 * d + 1]) for d in range(GROUP)]


def wide(value):
    return value.astype(jnp.float32)


def plus(a, b):
    return (a.astype(jnp.float32) + b.astype(jnp.float32)).astype(jnp.bfloat16)


def exchange(packed):
    experts = lax.axis_size("x")
    blocks = packed.reshape(experts, LANES, packed.shape[1])
    moved = lax.all_to_all(blocks, "x", split_axis=0, concat_axis=0, tiled=True)
    return moved.reshape(packed.shape)


def ring_sum(parts):
    right_a, left_b = shift(parts[4][0], 1), shift(parts[4][1], -1)
    right_b, left_a = shift(parts[3][1], 1), shift(parts[5][0], -1)
    for s in (3, 2, 1):
        right_a = shift(plus(right_a, parts[s][0]), 1)
        left_b = shift(plus(left_b, parts[GROUP - s][1]), -1)
        if s < 3:
            right_b = shift(plus(right_b, parts[s][1]), 1)
            left_a = shift(plus(left_a, parts[GROUP - s][0]), -1)
    first = wide(parts[0][0]) + wide(right_a) + wide(left_a)
    second = wide(parts[0][1]) + wide(right_b) + wide(left_b)
    return first.astype(jnp.bfloat16), second.astype(jnp.bfloat16)


def select(matrix, values):
    return jnp.dot(matrix, values, preferred_element_type=jnp.float32).astype(jnp.bfloat16)


def experts_of(packed, gate_w, up_w, down_w):
    experts = lax.axis_size("x")
    held = experts * SLOTS
    tall = -(-held // 8) * 8
    lane = jnp.arange(experts * LANES, dtype=jnp.int32)
    dense = jnp.where(lane % LANES < SLOTS, lane // LANES * SLOTS + lane % LANES, -1)
    spread = (dense[:, None] == jnp.arange(tall, dtype=jnp.int32)[None, :]).astype(jnp.bfloat16)
    mine = select(spread.T, exchange(packed))
    rows = lax.all_gather(mine.astype(jnp.float16), "y", axis=0, tiled=True)
    parts = expert_parts(rows.astype(jnp.bfloat16), gate_w, up_w, down_w)
    halves = [select(spread, half) for half in ring_sum(parts)]
    return exchange(jnp.concatenate(halves, axis=1))


def normalise(rows, gain):
    float_rows = wide(rows)
    variance = jnp.mean(float_rows * float_rows, axis=-1, keepdims=True)
    return (float_rows * lax.rsqrt(variance + 1e-06) * gain).astype(jnp.bfloat16)


def first_kernel(rows_ref, gain_ref, chosen_ref, packed_ref, pick_ref):
    count, rows = pick_ref.shape[1:]
    earlier = lax.broadcasted_iota(jnp.int32, (rows, rows), 0) < lax.broadcasted_iota(
        jnp.int32, (rows, rows), 1
    )
    earlier = earlier.astype(jnp.float32).astype(jnp.bfloat16)
    lane = lax.broadcasted_iota(jnp.int32, (count, rows), 0)
    for t in range(chosen_ref.shape[0]):
        chosen = jnp.broadcast_to(chosen_ref[t : t + 1, :], (8, rows))
        place = jnp.zeros((8, rows), jnp.float32)
        for e in range(count // LANES):
            mine = (chosen == e).astype(jnp.float32)
            before = jnp.dot(
                mine.astype(jnp.bfloat16), earlier, preferred_element_type=jnp.float32
            )
            place = place + mine * before
        slot = chosen * LANES + place.astype(jnp.int32)
        hit = lane == jnp.broadcast_to(slot[:1, :], (count, rows))
        pick_ref[t] = hit.astype(jnp.float32).astype(jnp.bfloat16)
    normed = normalise(rows_ref[...], gain_ref[...])
    packed_ref[...] = jnp.dot(
        pick_ref[0], normed, preferred_element_type=jnp.float32
    ).astype(jnp.bfloat16)


def first_step(rows, gain, chosen, count):
    ticks, row_count = chosen.shape
    width = rows.shape[1]
    return pl.pallas_call(
        first_kernel,
        out_shape=[
            jax.ShapeDtypeStruct((count, width), jnp.bfloat16),
            jax.ShapeDtypeStruct((ticks, count, row_count), jnp.bfloat16),
        ],
        in_specs=[pl.BlockSpec(memory_space=pltpu.VMEM)] * 3,
        out_specs=[pl.BlockSpec(memory_space=pltpu.VMEM)] * 2,
        compiler_params=pltpu.CompilerParams(vmem_limit_bytes=16 * 2**20),
    )(rows, gain, chosen)


def local(pending, incoming, gain, gate_w, up_w, down_w, chosen, scores):
    ticks, row_count = chosen.shape[0], chosen.shape[2]
    first_section = lax.axis_index("pp") == 0
    count = lax.axis_size("pp")
    rows = pending[0]
    packed, pick = first_step(
        rows, gain, chosen.reshape(ticks, row_count), lax.axis_size("x") * LANES
    )
    outputs = []
    for tick in range(ticks):
        if tick:
            packed = select(pick[tick], normalise(rows, gain))
        back = experts_of(packed, gate_w[0], up_w[0], down_w[0])
        combined = jnp.dot(pick[tick].T, back, preferred_element_type=jnp.float32)
        produced = (wide(rows) + scores[tick, 0] * combined).astype(jnp.bfloat16)
        outputs.append(produced)
        if tick + 1 < ticks:
            passed = lax.ppermute(produced, "pp", [(i, i + 1) for i in range(count - 1)])
            rows = jnp.where(first_section, incoming[tick], passed)
    return jnp.stack(outputs)[:, None]


def solution(mesh):
    fine = Mesh(mesh.devices.reshape(mesh.shape["pp"], -1, GROUP), ("pp", "x", "y"))
    ep = ("x", "y")
    in_specs = (
        P("pp", ep, None),
        P(None, ep, None),
        P("pp", None),
        P("pp", None, ep),
        P("pp", None, ep),
        P("pp", ep, None),
        P(None, "pp", ep, None),
        P(None, "pp", ep, None),
    )
    out_specs = P(None, "pp", ep, None)
    return jax.shard_map(local, mesh=fine, in_specs=in_specs, out_specs=out_specs, check_vma=False)
```
